32 devices in a mesh: gx: 2 (over x), gy: 4 (over y, core), gz: 4 (over z).
Axes of the slice: x: 2, y: 2, z: 4, core: 2. Of those that a mesh axis runs over, the one named last changes fastest.
Arguments:
- panel: float32 [128, 131072], P(None, ('gx', 'gy', 'gz')), may hold values from -3000 to 3000
- trailing: float32 [64, 131072], P(None, ('gx', 'gy', 'gz')), may hold values from -6 to 6
Outputs:
- basis: float32 [128, 131072], P(None, ('gx', 'gy', 'gz'))
- upper: float32 [128, 128], replicated
- coupling: float32 [128, 64], replicated
- updated: float32 [64, 131072], P(None, ('gx', 'gy', 'gz'))
The draws below stay inside these ranges and needn't reach their ends.
All inputs are finite; a program needn't handle non-finite values.
Results may differ from the reference program's by a relative error of at most 0.0033.
Values sent between devices are 32-bit elements; how exact they have to be, the bound alone decides.
A program may use at most 64 MiB of HBM per device.

```python
import jax
import jax.numpy as jnp
from jax import lax

P_SIZE = 128
TRAIL = 64
ROWS = 131072


def draw_panel(key, part):
    k_base, k_cols, k_rows, k_left, k_right, k_sing = jax.random.split(jax.random.fold_in(key, 17), 6)
    left_turn, _ = jnp.linalg.qr(jax.random.normal(k_left, (P_SIZE, P_SIZE), jnp.float32))
    right_turn, _ = jnp.linalg.qr(jax.random.normal(k_right, (P_SIZE, P_SIZE), jnp.float32))
    spread = jnp.log(500.0)
    place = jnp.arange(P_SIZE, dtype=jnp.int32)
    base = jax.random.truncated_normal(k_base, -4.0, 4.0, (P_SIZE, ROWS), jnp.float32)
    cols = jnp.exp(jax.random.uniform(k_cols, (P_SIZE, 1), jnp.float32, 0.0, jnp.log(10.0)))
    level = jax.random.uniform(k_sing, (P_SIZE,), jnp.float32, 0.0, 1.0)
    level = jnp.where(place == 0, 0.0, jnp.where(place == 1, 1.0, level))
    singular = jnp.exp(-spread * level)
    mixing = jnp.dot(left_turn * singular[None, :], right_turn, precision=lax.Precision.HIGHEST)
    mixed = 3.5 * jnp.dot(mixing, base, precision=lax.Precision.HIGHEST)
    rising = 1.0 + 2.0 * jnp.arange(ROWS, dtype=jnp.float32)[None, :] / ROWS
    rows = jnp.exp(jax.random.uniform(k_rows, (1, ROWS), jnp.float32, 0.0, jnp.log(10.0))) * rising
    return jnp.clip(mixed * cols * rows, -3000.0, 3000.0)


def block_levels(stream_key, shape, cuts, low, high):
    def one(axis_at, blocks):
        draws = jax.random.uniform(jax.random.fold_in(jax.random.fold_in(stream_key, 6), axis_at), (blocks,), jnp.float32, low / len(cuts), high / len(cuts))
        return jnp.repeat(jnp.exp(draws), shape[axis_at] // blocks).reshape((-1,) + (1,) * (len(shape) - axis_at - 1))

    level = one(*cuts[0])
    for cut in cuts[1:]:
        level = level * one(*cut)
    return level


def normal_values(stream_key, dims, scale, limit, cuts=(), kind=jnp.bfloat16):
    array = scale * jax.random.normal(stream_key, dims, jnp.float32)
    if cuts:
        array = array * block_levels(stream_key, dims, cuts, -0.22, 0.18)
    return jnp.clip(array, -limit, limit).astype(kind)


def setup_inputs(seed: int = 0) -> dict:
    seeds = jax.random.split(jax.random.key(seed), 3)
    panel = draw_panel(jax.random.fold_in(seeds[2], 71), 0)
    trailing = normal_values(seeds[1], (TRAIL, ROWS), 1.0, 6.0, ((1, 32),), jnp.float32)
    return {"panel": panel, "trailing": trailing}


def matmul(left, right):
    return jnp.dot(left.astype(jnp.float32), right.astype(jnp.float32), precision=lax.Precision.HIGHEST, preferred_element_type=jnp.float32)

def lower_solve(lower, rhs):
    return lax.linalg.triangular_solve(lower, rhs, left_side=True, lower=True)

def reference(panel, trailing):
    first_low = jnp.linalg.cholesky(matmul(panel, panel.T))
    first = lower_solve(first_low, panel)
    second_low = jnp.linalg.cholesky(matmul(first, first.T))
    basis_t = lower_solve(second_low, first)
    whole_low = matmul(first_low, second_low)
    coupling = matmul(basis_t, trailing.T)
    updated = trailing - matmul(coupling.T, basis_t)
    scale = jnp.sqrt(jnp.float32(ROWS))
    return (basis_t * scale, whole_low.T / scale, coupling, updated)
```

```python
import functools

import jax
import jax.numpy as jnp
from jax import lax
from jax.experimental import pallas as pl
from jax.experimental.pallas import tpu as pltpu
from jax.sharding import PartitionSpec as P

MESH = pl.DeviceIdType.MESH
HIGHEST = lax.Precision.HIGHEST
NT = (((1,), (1,)), ((), ()))
NN = (((1,), (0,)), ((), ()))
VMEM = pl.BlockSpec(memory_space=pltpu.VMEM)
ANY = pl.BlockSpec(memory_space=pl.ANY)


def exact(left, right, dims):
    return lax.dot_general(left, right, dims, precision=HIGHEST, preferred_element_type=jnp.float32)


def halves(value):
    high = value.astype(jnp.bfloat16)
    return high, (value - high.astype(jnp.float32)).astype(jnp.bfloat16)


def three_pass(left, right, dims):
    dot = functools.partial(lax.dot_general, dimension_numbers=dims, preferred_element_type=jnp.float32)
    return dot(left[0], right[1]) + dot(left[1], right[0]) + dot(left[0], right[0])


def factor(tiles):
    size = tiles[0].shape[1]
    lane = lax.broadcasted_iota(jnp.int32, (1, size), 1)
    row_in_tile = lax.broadcasted_iota(jnp.int32, (8, 1), 0)
    lanes = lax.broadcasted_iota(jnp.int32, (8, size), 1)
    tiles = list(tiles)
    for k in range(size):
        at, r = divmod(k, 8)
        row = tiles[at][r : r + 1, :]
        here = lanes == k
        scaled = jnp.where(lane == k, 1.0, row) * (1.0 / row[:, k : k + 1])
        for h in range(at, len(tiles)):
            if h == at and r == 7:
                continue
            tile = tiles[h]
            new = jnp.where(here, 0.0, tile) - tile[:, k : k + 1] * scaled
            tiles[h] = jnp.where(row_in_tile > r, new, tile) if h == at else new
    uppers, inverses = [], []
    for h, tile in enumerate(tiles):
        rows = row_in_tile + 8 * h
        pivot = jnp.sum(jnp.where(lanes == rows, tile, 0.0), axis=1, keepdims=True)
        root = jnp.sqrt(pivot)
        over = 1.0 / root
        uppers.append(jnp.where(lanes > rows, tile * over, jnp.where(lanes == rows, root, 0.0)))
        inverses.append(jnp.where(lanes < rows, tile * over, jnp.where(lanes == rows, over, 0.0)))
    return uppers, inverses


def greet(sizes):
    nx, ny, nz = sizes
    gx, gy, gz = lax.axis_index("gx"), lax.axis_index("gy"), lax.axis_index("gz")
    barrier = pltpu.get_barrier_semaphore()
    me = gx * ny + gy
    for step in range(1, nx * ny):
        peer = lax.rem(me + step, nx * ny)
        pl.semaphore_signal(barrier, inc=1, device_id=(peer // ny, lax.rem(peer, ny), gz), device_id_type=MESH)
    for step in range(1, nz):
        pl.semaphore_signal(barrier, inc=1, device_id=(gx, gy, lax.rem(gz + step, nz)), device_id_type=MESH)


def all_sum(sizes, send, landed, column, gathered, send_sem, recv_sem):
    nx, ny, nz = sizes
    group = nx * ny
    gx, gy, gz = lax.axis_index("gx"), lax.axis_index("gy"), lax.axis_index("gz")
    me = gx * ny + gy
    pl.semaphore_wait(pltpu.get_barrier_semaphore(), group - 1 + nz - 1)

    def plane_copy(src, dst, step, base):
        peer = lax.rem(me + step, group)
        return pltpu.make_async_remote_copy(
            src_ref=src(peer),
            dst_ref=dst,
            send_sem=send_sem.at[base + step],
            recv_sem=recv_sem.at[base + step],
            device_id=(peer // ny, lax.rem(peer, ny), gz),
            device_id_type=MESH,
        )

    out = [plane_copy(lambda peer: send.at[peer], landed.at[step], step, 0) for step in range(1, group)]
    for copy in out:
        copy.start()
    part = send[me]
    for step in range(1, group):
        out[step - 1].wait_recv()
        part = part + landed[step]
    column[gz] = part
    along = [
        pltpu.make_async_remote_copy(
            src_ref=column.at[gz],
            dst_ref=column.at[gz],
            send_sem=send_sem.at[group + step],
            recv_sem=recv_sem.at[group + step],
            device_id=(gx, gy, lax.rem(gz + step, nz)),
            device_id_type=MESH,
        )
        for step in range(1, nz)
    ]
    for copy in along:
        copy.start()
    for copy in along:
        copy.wait_recv()
    total = column[0]
    for z in range(1, nz):
        total = total + column[z]
    gathered[me] = total
    back = [plane_copy(lambda peer: gathered.at[me], gathered.at[me], step, group + nz) for step in range(1, group)]
    for copy in back:
        copy.start()
    for copy in back:
        copy.wait_recv()
    for copy in out + along + back:
        copy.wait_send()


def sum_scratch(sizes, rows, size):
    nx, ny, nz = sizes
    group = nx * ny
    return [
        pltpu.VMEM((group, rows, size), jnp.float32),
        pltpu.VMEM((group, rows, size), jnp.float32),
        pltpu.VMEM((nz, rows, size), jnp.float32),
        pltpu.SemaphoreType.DMA((2 * group + nz,)),
        pltpu.SemaphoreType.DMA((2 * group + nz,)),
    ]


def chunk_of(width):
    return 512 if width % 512 == 0 else width


def gram_kernel(sizes, panel, gathered, send, landed, column, send_sem, recv_sem):
    greet(sizes)
    size, width = panel.shape
    chunk = chunk_of(width)

    def body(i, total):
        part = panel[:, pl.ds(pl.multiple_of(i * chunk, chunk), chunk)]
        return total + exact(part, part, NT)

    gram = lax.fori_loop(0, width // chunk, body, jnp.zeros((size, size), jnp.float32))
    group = sizes[0] * sizes[1]
    rows = size // group
    for p in range(group):
        send[p] = gram[p * rows : (p + 1) * rows]
    all_sum(sizes, send, landed, column, gathered, send_sem, recv_sem)


def factor_kernel(gram, upper, inverse):
    uppers, inverses = factor([gram[h : h + 8] for h in range(0, gram.shape[0], 8)])
    for h in range(len(uppers)):
        upper[8 * h : 8 * h + 8] = uppers[h]
        inverse[8 * h : 8 * h + 8] = inverses[h]


def apply_kernel(sizes, inverse, panel, trailing, first, gathered, send, landed, column, send_sem, recv_sem):
    greet(sizes)
    size, width = panel.shape
    trail = trailing.shape[0]
    chunk = chunk_of(width)
    inv = inverse[...]

    def body(i, totals):
        at = pl.ds(pl.multiple_of(i * chunk, chunk), chunk)
        basis = exact(inv, panel[:, at], NN)
        first[:, at] = basis
        high, low = halves(basis)
        own, cross = totals
        own = own + three_pass((high, low), (high, low), NT)
        cross = cross + three_pass(halves(trailing[:, at]), (high, low), NT)
        return own, cross

    start = (jnp.zeros((size, size), jnp.float32), jnp.zeros((trail, size), jnp.float32))
    own, cross = lax.fori_loop(0, width // chunk, body, start)
    group = sizes[0] * sizes[1]
    rows, less = size // group, trail // group
    for p in range(group):
        send[p, :rows] = own[p * rows : (p + 1) * rows]
        send[p, rows:] = cross[p * less : (p + 1) * less]
    all_sum(sizes, send, landed, column, gathered, send_sem, recv_sem)


def final_kernel(scale, gram, cross, upper_one, first, trailing, basis, upper, coupling, updated):
    size, width = first.shape
    uppers, inverses = factor([gram[h : h + 8] for h in range(0, size, 8)])
    inv = jnp.concatenate(inverses, axis=0)
    up = jnp.concatenate(uppers, axis=0)
    upper[...] = exact(up, upper_one[...], NN) * (1.0 / scale)
    coupling[...] = exact(inv, cross[...], NT)
    back = exact(exact(cross[...], inv, NT), inv, NN)
    scaled_inv, back = halves(inv * scale), halves(back)
    chunk = chunk_of(width)

    @pl.loop(0, width // chunk)
    def _(i):
        at = pl.ds(pl.multiple_of(i * chunk, chunk), chunk)
        part = halves(first[:, at])
        basis[:, at] = three_pass(scaled_inv, part, NN)
        updated[:, at] = trailing[:, at] - three_pass(back, part, NN)


def shards(sizes, panel, trailing):
    size, width = panel.shape
    trail = trailing.shape[0]
    nx, ny, nz = sizes
    group = nx * ny
    rows, less = size // group, trail // group
    f32 = jnp.float32
    scale = float(width * group * nz) ** 0.5

    def params(identity=None):
        return pltpu.CompilerParams(collective_id=identity, has_side_effects=identity is not None, vmem_limit_bytes=48 * 2**20)

    gram = pl.pallas_call(
        functools.partial(gram_kernel, sizes),
        out_shape=jax.ShapeDtypeStruct((group, rows, size), f32),
        in_specs=[VMEM],
        out_specs=VMEM,
        scratch_shapes=sum_scratch(sizes, rows, size),
        compiler_params=params(0),
        name="gram",
    )(panel)
    upper_one, inverse_one = pl.pallas_call(
        factor_kernel,
        out_shape=[jax.ShapeDtypeStruct((size, size), f32)] * 2,
        in_specs=[VMEM],
        out_specs=[VMEM] * 2,
        compiler_params=params(),
        name="factor",
    )(gram.reshape(size, size))
    first, summed = pl.pallas_call(
        functools.partial(apply_kernel, sizes),
        out_shape=[jax.ShapeDtypeStruct((size, width), f32), jax.ShapeDtypeStruct((group, rows + less, size), f32)],
        in_specs=[VMEM] * 3,
        out_specs=[VMEM] * 2,
        scratch_shapes=sum_scratch(sizes, rows + less, size),
        compiler_params=params(1),
        name="apply",
    )(inverse_one, panel, trailing)
    return pl.pallas_call(
        functools.partial(final_kernel, scale),
        out_shape=[
            jax.ShapeDtypeStruct((size, width), f32),
            jax.ShapeDtypeStruct((size, size), f32),
            jax.ShapeDtypeStruct((size, trail), f32),
            jax.ShapeDtypeStruct((trail, width), f32),
        ],
        in_specs=[VMEM] * 5,
        out_specs=[VMEM] * 4,
        compiler_params=params(),
        name="final",
    )(summed[:, :rows].reshape(size, size), summed[:, rows:].reshape(trail, size), upper_one, first, trailing)


def solution(mesh):
    sizes = tuple(mesh.shape[name] for name in ("gx", "gy", "gz"))
    placed = P(None, ("gx", "gy", "gz"))
    return jax.shard_map(
        functools.partial(shards, sizes),
        mesh=mesh,
        in_specs=(placed, placed),
        out_specs=(placed, P(), P(), placed),
        check_vma=False,
    )
```

```python
import functools

import jax
import jax.numpy as jnp
from jax import lax
from jax.experimental import pallas as pl
from jax.experimental.pallas import tpu as pltpu
from jax.sharding import PartitionSpec as P

MESH = pl.DeviceIdType.MESH
HIGHEST = lax.Precision.HIGHEST
NT = (((1,), (1,)), ((), ()))
NN = (((1,), (0,)), ((), ()))
VMEM = pl.BlockSpec(memory_space=pltpu.VMEM)
HBM = pl.BlockSpec(memory_space=pltpu.HBM)


def exact(left, right, dims):
    return lax.dot_general(left, right, dims, precision=HIGHEST, preferred_element_type=jnp.float32)


def terms(value, count):
    found = []
    for _ in range(count):
        term = value.astype(jnp.bfloat16)
        found.append(term)
        value = value - term.astype(jnp.float32)
    return found


def stacked(left, right, dims):
    return lax.dot_general(left, right, dims, preferred_element_type=jnp.float32)


def factor(tiles):
    size = tiles[0].shape[1]
    lane = lax.broadcasted_iota(jnp.int32, (1, size), 1)
    row_in_tile = lax.broadcasted_iota(jnp.int32, (8, 1), 0)
    lanes = lax.broadcasted_iota(jnp.int32, (8, size), 1)
    tiles = list(tiles)
    for at in range(len(tiles)):
        first = 8 * at
        inside = (lane >= first) & (lane < first + 8)
        columns = {h: [jnp.broadcast_to(tiles[h][:, first + j : first + j + 1], (8, size)) for j in range(8)] for h in range(at, len(tiles))}
        for h in range(at + 1, len(tiles)):
            tiles[h] = jnp.where(inside, 0.0, tiles[h])
        for r in range(8):
            k = first + r
            row = tiles[at][r : r + 1, :]
            unit = jnp.where(lane == k, 1.0, row)
            behind = jnp.where(inside & (lane > k), 0.0, unit)
            pivots = [columns[at][j][r : r + 1, :] for j in range(8)]
            over = 1.0 / pivots[r]
            for h in range(at, len(tiles)):
                if h == at and r == 7:
                    continue
                times = columns[h][r] * over
                for j in range(r + 1, 8):
                    columns[h][j] = columns[h][j] - times * pivots[j]
                if h == at:
                    below = row_in_tile > r
                    tiles[h] = jnp.where(below, jnp.where(lanes == k, 0.0, tiles[h]) - times * unit, tiles[h])
                else:
                    tiles[h] = tiles[h] - times * behind
    uppers, inverses = [], []
    for h, tile in enumerate(tiles):
        rows = row_in_tile + 8 * h
        pivot = jnp.sum(jnp.where(lanes == rows, tile, 0.0), axis=1, keepdims=True)
        root = jnp.sqrt(pivot)
        over = 1.0 / root
        uppers.append(jnp.where(lanes > rows, tile * over, jnp.where(lanes == rows, root, 0.0)))
        inverses.append(jnp.where(lanes < rows, tile * over, jnp.where(lanes == rows, over, 0.0)))
    return uppers, inverses


def greet(sizes):
    nx, ny, nz = sizes
    gx, gy, gz = lax.axis_index("gx"), lax.axis_index("gy"), lax.axis_index("gz")
    barrier = pltpu.get_barrier_semaphore()
    me = gx * ny + gy
    for step in range(1, nx * ny):
        peer = lax.rem(me + step, nx * ny)
        pl.semaphore_signal(barrier, inc=1, device_id=(peer // ny, lax.rem(peer, ny), gz), device_id_type=MESH)
    for step in range(1, nz):
        pl.semaphore_signal(barrier, inc=1, device_id=(gx, gy, lax.rem(gz + step, nz)), device_id_type=MESH)


def all_sum(sizes, send, landed, column, gathered, send_sem, recv_sem):
    nx, ny, nz = sizes
    group = nx * ny
    gx, gy, gz = lax.axis_index("gx"), lax.axis_index("gy"), lax.axis_index("gz")
    me = gx * ny + gy
    pl.semaphore_wait(pltpu.get_barrier_semaphore(), group - 1 + nz - 1)

    def plane_copy(src, dst, step, base):
        peer = lax.rem(me + step, group)
        return pltpu.make_async_remote_copy(
            src_ref=src(peer),
            dst_ref=dst,
            send_sem=send_sem.at[base + step],
            recv_sem=recv_sem.at[base + step],
            device_id=(peer // ny, lax.rem(peer, ny), gz),
            device_id_type=MESH,
        )

    out = [plane_copy(lambda peer: send.at[peer], landed.at[step], step, 0) for step in range(1, group)]
    for copy in out:
        copy.start()
    part = send[me]
    for step in range(1, group):
        out[step - 1].wait_recv()
        part = part + landed[step]
    column[gz] = part
    along = [
        pltpu.make_async_remote_copy(
            src_ref=column.at[gz],
            dst_ref=column.at[gz],
            send_sem=send_sem.at[group + step],
            recv_sem=recv_sem.at[group + step],
            device_id=(gx, gy, lax.rem(gz + step, nz)),
            device_id_type=MESH,
        )
        for step in range(1, nz)
    ]
    for copy in along:
        copy.start()
    for copy in along:
        copy.wait_recv()
    total = column[0]
    for z in range(1, nz):
        total = total + column[z]
    gathered[me] = total
    back = [plane_copy(lambda peer: gathered.at[me], gathered.at[me], step, group + nz) for step in range(1, group)]
    for copy in back:
        copy.start()
    for copy in back:
        copy.wait_recv()
    for copy in out + along + back:
        copy.wait_send()


def sum_scratch(sizes, rows, size):
    nx, ny, nz = sizes
    group = nx * ny
    return [
        pltpu.VMEM((group, rows, size), jnp.float32),
        pltpu.VMEM((group, rows, size), jnp.float32),
        pltpu.VMEM((nz, rows, size), jnp.float32),
        pltpu.SemaphoreType.DMA((2 * group + nz,)),
        pltpu.SemaphoreType.DMA((2 * group + nz,)),
    ]


def chunk_of(width, most):
    return most if width % most == 0 else width


def gram_kernel(sizes, panel, gathered, held, load_sem, send, landed, column, send_sem, recv_sem):
    size, width = panel.shape
    chunk = chunk_of(width, 1024)
    loads = []
    for i in range(width // chunk):
        at = pl.ds(i * chunk, chunk)
        loads.append(pltpu.make_async_copy(panel.at[:, at], held.at[:, at], load_sem.at[i]))
        loads[-1].start()
    greet(sizes)
    both = jnp.zeros((2 * size, 2 * size), jnp.float32)
    small = jnp.zeros((size, size), jnp.float32)
    for i in range(width // chunk):
        loads[i].wait()
        high, middle, low = terms(held[:, i * chunk : (i + 1) * chunk], 3)
        pair = jnp.concatenate([high, middle], axis=0)
        both = both + stacked(pair, pair, NT)
        small = small + stacked(high, low, NT)
    small = small + both[:size, size:]
    gram = both[:size, :size] + ((small + small.T) + both[size:, size:])
    group = sizes[0] * sizes[1]
    rows = size // group
    for p in range(group):
        send[p] = gram[p * rows : (p + 1) * rows]
    all_sum(sizes, send, landed, column, gathered, send_sem, recv_sem)


def factor_kernel(gram, trailing, upper, inverse, near, load_sem):
    load = pltpu.make_async_copy(trailing, near, load_sem)
    load.start()
    uppers, inverses = factor([gram[h : h + 8] for h in range(0, gram.shape[0], 8)])
    for h in range(len(uppers)):
        upper[8 * h : 8 * h + 8] = uppers[h]
        inverse[8 * h : 8 * h + 8] = inverses[h]
    load.wait()


def apply_kernel(sizes, inverse, panel, trailing, first, gathered, send, landed, column, send_sem, recv_sem):
    greet(sizes)
    size, width = panel.shape
    trail = trailing.shape[0]
    chunk = chunk_of(width, 1024)
    one, two, three = terms(inverse[...], 3)
    left = jnp.concatenate([three, one, two, two, one, one], axis=1)

    def body(i, total):
        at = pl.ds(pl.multiple_of(i * chunk, chunk), chunk)
        high, middle, low = terms(panel[:, at], 3)
        basis = stacked(left, jnp.concatenate([high, low, middle, high, middle, high], axis=0), NN)
        first[:, at] = basis
        high, low = terms(basis, 2)
        c_high, c_low = terms(trailing[:, at], 2)
        pairs = stacked(jnp.concatenate([high, c_high, c_low], axis=0), jnp.concatenate([high, low], axis=0), NT)
        return total + pairs

    total = lax.fori_loop(0, width // chunk, body, jnp.zeros((size + 2 * trail, 2 * size), jnp.float32))
    mixed = total[:size, size:]
    own = total[:size, :size] + (mixed + mixed.T)
    cross = total[size:, :size] + total[size:, size:]
    cross = cross[:trail] + cross[trail:]
    group = sizes[0] * sizes[1]
    rows, less = size // group, trail // group
    for p in range(group):
        send[p, :rows] = own[p * rows : (p + 1) * rows]
        send[p, rows:] = cross[p * less : (p + 1) * less]
    all_sum(sizes, send, landed, column, gathered, send_sem, recv_sem)


def final_kernel(scale, gram, cross, upper_one, first, trailing, basis, upper, coupling, updated, basis_held, updated_held, store_sem):
    size, width = first.shape
    uppers, inverses = factor([gram[h : h + 8] for h in range(0, size, 8)])
    inv = jnp.concatenate(inverses, axis=0)
    up = jnp.concatenate(uppers, axis=0)
    mixed = exact(cross[...], inv, NT)
    coupling[...] = mixed
    both = jnp.concatenate([inv * scale, exact(mixed, inv, NN)], axis=0)
    high, low = terms(both, 2)
    left = jnp.concatenate([low, low, high, high], axis=1)
    chunk = chunk_of(width, 512)
    stores = []
    for i in range(width // chunk):
        at = pl.ds(i * chunk, chunk)
        high, low = terms(first[:, at], 2)
        out = stacked(left, jnp.concatenate([low, high, low, high], axis=0), NN)
        basis_held[:, at] = out[:size]
        updated_held[:, at] = trailing[:, at] - out[size:]
        for place, (src, dst) in enumerate(((basis_held, basis), (updated_held, updated))):
            stores.append(pltpu.make_async_copy(src.at[:, at], dst.at[:, at], store_sem.at[place, i]))
            stores[-1].start()
    upper[...] = exact(up, upper_one[...], NN) * (1.0 / scale)
    for store in stores:
        store.wait()


def shards(sizes, panel, trailing):
    size, width = panel.shape
    trail = trailing.shape[0]
    nx, ny, nz = sizes
    group = nx * ny
    rows, less = size // group, trail // group
    f32 = jnp.float32
    scale = float(width * group * nz) ** 0.5

    def params(identity=None):
        return pltpu.CompilerParams(collective_id=identity, has_side_effects=identity is not None, vmem_limit_bytes=48 * 2**20)

    gram = pl.pallas_call(
        functools.partial(gram_kernel, sizes),
        out_shape=jax.ShapeDtypeStruct((group, rows, size), f32),
        in_specs=[HBM],
        out_specs=VMEM,
        scratch_shapes=[
            pltpu.VMEM((size, width), f32),
            pltpu.SemaphoreType.DMA((width // chunk_of(width, 1024),)),
            *sum_scratch(sizes, rows, size),
        ],
        compiler_params=params(0),
        name="gram",
    )(panel)
    upper_one, inverse_one, near = pl.pallas_call(
        factor_kernel,
        out_shape=[jax.ShapeDtypeStruct((size, size), f32)] * 2 + [jax.ShapeDtypeStruct((trail, width), f32)],
        in_specs=[VMEM, HBM],
        out_specs=[VMEM] * 3,
        scratch_shapes=[pltpu.SemaphoreType.DMA],
        compiler_params=params(),
        name="factor",
    )(gram.reshape(size, size), trailing)
    first, summed = pl.pallas_call(
        functools.partial(apply_kernel, sizes),
        out_shape=[jax.ShapeDtypeStruct((size, width), f32), jax.ShapeDtypeStruct((group, rows + less, size), f32)],
        in_specs=[VMEM] * 3,
        out_specs=[VMEM] * 2,
        scratch_shapes=sum_scratch(sizes, rows + less, size),
        compiler_params=params(1),
        name="apply",
    )(inverse_one, panel, near)
    basis, upper, coupling_t, updated = pl.pallas_call(
        functools.partial(final_kernel, scale),
        out_shape=[
            jax.ShapeDtypeStruct((size, width), f32),
            jax.ShapeDtypeStruct((size, size), f32),
            jax.ShapeDtypeStruct((trail, size), f32),
            jax.ShapeDtypeStruct((trail, width), f32),
        ],
        in_specs=[VMEM] * 5,
        out_specs=[HBM, VMEM, VMEM, HBM],
        scratch_shapes=[
            pltpu.VMEM((size, width), f32),
            pltpu.VMEM((trail, width), f32),
            pltpu.SemaphoreType.DMA((2, width // chunk_of(width, 512))),
        ],
        compiler_params=params(),
        name="final",
    )(summed[:, :rows].reshape(size, size), summed[:, rows:].reshape(trail, size), upper_one, first, near)
    return basis, upper, coupling_t.T, updated


def solution(mesh):
    sizes = tuple(mesh.shape[name] for name in ("gx", "gy", "gz"))
    placed = P(None, ("gx", "gy", "gz"))
    return jax.shard_map(
        functools.partial(shards, sizes),
        mesh=mesh,
        in_specs=(placed, placed),
        out_specs=(placed, P(), P(), placed),
        check_vma=False,
    )
```

```python
import functools

import jax
import jax.numpy as jnp
from jax import lax
from jax.experimental import pallas as pl
from jax.experimental.pallas import tpu as pltpu
from jax.sharding import PartitionSpec as P

MESH = pl.DeviceIdType.MESH
HIGHEST = lax.Precision.HIGHEST
NT = (((1,), (1,)), ((), ()))
NN = (((1,), (0,)), ((), ()))
VMEM = pl.BlockSpec(memory_space=pltpu.VMEM)
HBM = pl.BlockSpec(memory_space=pltpu.HBM)


def exact(left, right, dims):
    return lax.dot_general(left, right, dims, precision=HIGHEST, preferred_element_type=jnp.float32)


def terms(value, count):
    found = []
    for _ in range(count):
        term = value.astype(jnp.bfloat16)
        found.append(term)
        value = value - term.astype(jnp.float32)
    return found


def stacked(left, right, dims):
    return lax.dot_general(left, right, dims, preferred_element_type=jnp.float32)


def factor(tiles):
    size = tiles[0].shape[1]
    lane = lax.broadcasted_iota(jnp.int32, (1, size), 1)
    row_in_tile = lax.broadcasted_iota(jnp.int32, (8, 1), 0)
    lanes = lax.broadcasted_iota(jnp.int32, (8, size), 1)
    tiles = list(tiles)
    for at in range(len(tiles)):
        first = 8 * at
        inside = (lane >= first) & (lane < first + 8)
        columns = {h: [jnp.broadcast_to(tiles[h][:, first + j : first + j + 1], (8, size)) for j in range(8)] for h in range(at, len(tiles))}
        for h in range(at + 1, len(tiles)):
            tiles[h] = jnp.where(inside, 0.0, tiles[h])
        for r in range(8):
            k = first + r
            row = tiles[at][r : r + 1, :]
            unit = jnp.where(lane == k, 1.0, row)
            behind = jnp.where(inside & (lane > k), 0.0, unit)
            pivots = [columns[at][j][r : r + 1, :] for j in range(8)]
            over = 1.0 / pivots[r]
            for h in range(at, len(tiles)):
                if h == at and r == 7:
                    continue
                times = columns[h][r] * over
                for j in range(r + 1, 8):
                    columns[h][j] = columns[h][j] - times * pivots[j]
                if h == at:
                    below = row_in_tile > r
                    tiles[h] = jnp.where(below, jnp.where(lanes == k, 0.0, tiles[h]) - times * unit, tiles[h])
                else:
                    tiles[h] = tiles[h] - times * behind
    uppers, inverses = [], []
    for h, tile in enumerate(tiles):
        rows = row_in_tile + 8 * h
        pivot = jnp.sum(jnp.where(lanes == rows, tile, 0.0), axis=1, keepdims=True)
        root = jnp.sqrt(pivot)
        over = 1.0 / root
        uppers.append(jnp.where(lanes > rows, tile * over, jnp.where(lanes == rows, root, 0.0)))
        inverses.append(jnp.where(lanes < rows, tile * over, jnp.where(lanes == rows, over, 0.0)))
    return uppers, inverses


def greet(sizes):
    nx, ny, nz = sizes
    gx, gy, gz = lax.axis_index("gx"), lax.axis_index("gy"), lax.axis_index("gz")
    barrier = pltpu.get_barrier_semaphore()
    me = gx * ny + gy
    for step in range(1, nx * ny):
        peer = lax.rem(me + step, nx * ny)
        pl.semaphore_signal(barrier, inc=1, device_id=(peer // ny, lax.rem(peer, ny), gz), device_id_type=MESH)
    for step in range(1, nz):
        pl.semaphore_signal(barrier, inc=1, device_id=(gx, gy, lax.rem(gz + step, nz)), device_id_type=MESH)


def all_sum(sizes, send, landed, column, gathered, send_sem, recv_sem):
    nx, ny, nz = sizes
    group = nx * ny
    gx, gy, gz = lax.axis_index("gx"), lax.axis_index("gy"), lax.axis_index("gz")
    me = gx * ny + gy

    def plane_copy(src, dst, step, base):
        peer = lax.rem(me + step, group)
        return pltpu.make_async_remote_copy(
            src_ref=src(peer),
            dst_ref=dst,
            send_sem=send_sem.at[base + step],
            recv_sem=recv_sem.at[base + step],
            device_id=(peer // ny, lax.rem(peer, ny), gz),
            device_id_type=MESH,
        )

    out = [plane_copy(lambda peer: send.at[peer], landed.at[step], step, 0) for step in range(1, group)]
    for copy in out:
        copy.start()
    part = send[me]
    for step in range(1, group):
        out[step - 1].wait_recv()
        part = part + landed[step]
    column[gz] = part
    along = [
        pltpu.make_async_remote_copy(
            src_ref=column.at[gz],
            dst_ref=column.at[gz],
            send_sem=send_sem.at[group + step],
            recv_sem=recv_sem.at[group + step],
            device_id=(gx, gy, lax.rem(gz + step, nz)),
            device_id_type=MESH,
        )
        for step in range(1, nz)
    ]
    for copy in along:
        copy.start()
    for copy in along:
        copy.wait_recv()
    total = column[0]
    for z in range(1, nz):
        total = total + column[z]
    gathered[me] = total
    back = [plane_copy(lambda peer: gathered.at[me], gathered.at[me], step, group + nz) for step in range(1, group)]
    for copy in back:
        copy.start()
    for copy in back:
        copy.wait_recv()
    for copy in out + along + back:
        copy.wait_send()


def sum_scratch(sizes, rows, size):
    nx, ny, nz = sizes
    group = nx * ny
    return [
        pltpu.VMEM((group, rows, size), jnp.float32),
        pltpu.VMEM((group, rows, size), jnp.float32),
        pltpu.VMEM((nz, rows, size), jnp.float32),
        pltpu.SemaphoreType.DMA((2 * group + nz,)),
        pltpu.SemaphoreType.DMA((2 * group + nz,)),
    ]


def chunk_of(width, most):
    return most if width % most == 0 else width


def reduce_kernel(sizes, panel, trailing, first, upper, summed, panel_held, trailing_held, first_held, move_sem, *scratch):
    size, width = panel.shape
    trail = trailing.shape[0]
    group = sizes[0] * sizes[1]
    rows, less = size // group, trail // group
    chunk = chunk_of(width, 1024)
    greet(sizes)
    loads, more, stores = [], [], []
    for i in range(width // chunk):
        at = pl.ds(i * chunk, chunk)
        loads.append(pltpu.make_async_copy(panel.at[:, at], panel_held.at[:, at], move_sem.at[0, i]))
        loads[-1].start()
    for i in range(width // chunk):
        at = pl.ds(i * chunk, chunk)
        more.append(pltpu.make_async_copy(trailing.at[:, at], trailing_held.at[:, at], move_sem.at[1, i]))
        more[-1].start()
    both = jnp.zeros((2 * size, 2 * size), jnp.float32)
    small = jnp.zeros((size, size), jnp.float32)
    for i in range(width // chunk):
        loads[i].wait()
        high, middle, low = terms(panel_held[:, i * chunk : (i + 1) * chunk], 3)
        pair = jnp.concatenate([high, middle], axis=0)
        both = both + stacked(pair, pair, NT)
        small = small + stacked(high, low, NT)
    small = small + both[:size, size:]
    gram = both[:size, :size] + ((small + small.T) + both[size:, size:])
    gathered, *first_sum = scratch[:6]
    for p in range(group):
        first_sum[0][p] = gram[p * rows : (p + 1) * rows]
    pl.semaphore_wait(pltpu.get_barrier_semaphore(), group - 1 + sizes[2] - 1)
    all_sum(sizes, first_sum[0], first_sum[1], first_sum[2], gathered, *first_sum[3:])
    gram = jnp.concatenate([gathered[p] for p in range(group)], axis=0)
    uppers, inverses = factor([gram[h : h + 8] for h in range(0, size, 8)])
    for h in range(len(uppers)):
        upper[8 * h : 8 * h + 8] = uppers[h]
    inverse = jnp.concatenate(inverses, axis=0)
    one, two, three = terms(inverse, 3)
    left = jnp.concatenate([three, one, two, two, one, one], axis=1)
    total = jnp.zeros((size + 2 * trail, 2 * size), jnp.float32)
    for i in range(width // chunk):
        at = pl.ds(i * chunk, chunk)
        high, middle, low = terms(panel_held[:, at], 3)
        basis = stacked(left, jnp.concatenate([high, low, middle, high, middle, high], axis=0), NN)
        first_held[:, at] = basis
        stores.append(pltpu.make_async_copy(first_held.at[:, at], first.at[:, at], move_sem.at[2, i]))
        stores[-1].start()
        high, low = terms(basis, 2)
        more[i].wait()
        c_high, c_low = terms(trailing_held[:, at], 2)
        left_terms = jnp.concatenate([high, c_high, c_low], axis=0)
        total = total + stacked(left_terms, jnp.concatenate([high, low], axis=0), NT)
    mixed = total[:size, size:]
    own = total[:size, :size] + (mixed + mixed.T)
    cross = total[size:, :size] + total[size:, size:]
    cross = cross[:trail] + cross[trail:]
    second_sum = scratch[6:]
    for p in range(group):
        second_sum[0][p, :rows] = own[p * rows : (p + 1) * rows]
        second_sum[0][p, rows:] = cross[p * less : (p + 1) * less]
    all_sum(sizes, second_sum[0], second_sum[1], second_sum[2], summed, *second_sum[3:])
    for store in stores:
        store.wait()


def final_kernel(scale, summed, upper_one, first, trailing, basis, upper, coupling, updated, first_held, trailing_held, basis_held, updated_held, load_sem, store_sem):
    size, width = first.shape
    loads = [
        pltpu.make_async_copy(first, first_held, load_sem.at[0]),
        pltpu.make_async_copy(trailing, trailing_held, load_sem.at[1]),
    ]
    for load in loads:
        load.start()
    group = summed.shape[0]
    rows = size // group
    gram = jnp.concatenate([summed[p, :rows] for p in range(group)], axis=0)
    cross = jnp.concatenate([summed[p, rows:] for p in range(group)], axis=0)
    uppers, inverses = factor([gram[h : h + 8] for h in range(0, size, 8)])
    inv = jnp.concatenate(inverses, axis=0)
    up = jnp.concatenate(uppers, axis=0)
    mixed = exact(cross, inv, NT)
    coupling[...] = mixed
    both = jnp.concatenate([inv * scale, exact(mixed, inv, NN)], axis=0)
    high, low = terms(both, 2)
    left = jnp.concatenate([low, low, high, high], axis=1)
    chunk = chunk_of(width, 512)
    stores = []
    for load in loads:
        load.wait()
    for i in range(width // chunk):
        at = pl.ds(i * chunk, chunk)
        high, low = terms(first_held[:, at], 2)
        out = stacked(left, jnp.concatenate([low, high, low, high], axis=0), NN)
        basis_held[:, at] = out[:size]
        updated_held[:, at] = trailing_held[:, at] - out[size:]
        for place, (src, dst) in enumerate(((basis_held, basis), (updated_held, updated))):
            stores.append(pltpu.make_async_copy(src.at[:, at], dst.at[:, at], store_sem.at[place, i]))
            stores[-1].start()
    upper[...] = exact(up, upper_one[...], NN) * (1.0 / scale)
    for store in stores:
        store.wait()


def shards(sizes, panel, trailing):
    size, width = panel.shape
    trail = trailing.shape[0]
    nx, ny, nz = sizes
    group = nx * ny
    rows, less = size // group, trail // group
    f32 = jnp.float32
    scale = float(width * group * nz) ** 0.5

    def params(identity=None, mebibytes=63):
        return pltpu.CompilerParams(
            collective_id=identity, has_side_effects=identity is not None, vmem_limit_bytes=mebibytes * 2**20
        )

    first, upper_one, summed = pl.pallas_call(
        functools.partial(reduce_kernel, sizes),
        out_shape=[
            jax.ShapeDtypeStruct((size, width), f32),
            jax.ShapeDtypeStruct((size, size), f32),
            jax.ShapeDtypeStruct((group, rows + less, size), f32),
        ],
        in_specs=[HBM, HBM],
        out_specs=[HBM, VMEM, VMEM],
        scratch_shapes=[
            pltpu.VMEM((size, width), f32),
            pltpu.VMEM((trail, width), f32),
            pltpu.VMEM((size, width), f32),
            pltpu.SemaphoreType.DMA((3, width // chunk_of(width, 1024))),
            pltpu.VMEM((group, rows, size), f32),
            *sum_scratch(sizes, rows, size),
            *sum_scratch(sizes, rows + less, size),
        ],
        compiler_params=params(0),
        name="reduce",
    )(panel, trailing)
    basis, upper, coupling_t, updated = pl.pallas_call(
        functools.partial(final_kernel, scale),
        out_shape=[
            jax.ShapeDtypeStruct((size, width), f32),
            jax.ShapeDtypeStruct((size, size), f32),
            jax.ShapeDtypeStruct((trail, size), f32),
            jax.ShapeDtypeStruct((trail, width), f32),
        ],
        in_specs=[VMEM, VMEM, HBM, HBM],
        out_specs=[HBM, VMEM, VMEM, HBM],
        scratch_shapes=[
            pltpu.VMEM((size, width), f32),
            pltpu.VMEM((trail, width), f32),
            pltpu.VMEM((size, width), f32),
            pltpu.VMEM((trail, width), f32),
            pltpu.SemaphoreType.DMA((2,)),
            pltpu.SemaphoreType.DMA((2, width // chunk_of(width, 512))),
        ],
        compiler_params=params(),
        name="final",
    )(summed, upper_one, first, trailing)
    return basis, upper, coupling_t.T, updated


def solution(mesh):
    sizes = tuple(mesh.shape[name] for name in ("gx", "gy", "gz"))
    placed = P(None, ("gx", "gy", "gz"))
    return jax.shard_map(
        functools.partial(shards, sizes),
        mesh=mesh,
        in_specs=(placed, placed),
        out_specs=(placed, P(), P(), placed),
        check_vma=False,
    )
```

```python
import functools

import jax
import jax.numpy as jnp
from jax import lax
from jax.experimental import pallas as pl
from jax.experimental.pallas import tpu as pltpu
from jax.sharding import PartitionSpec as P

MESH = pl.DeviceIdType.MESH
HIGHEST = lax.Precision.HIGHEST
NT = (((1,), (1,)), ((), ()))
NN = (((1,), (0,)), ((), ()))
VMEM = pl.BlockSpec(memory_space=pltpu.VMEM)
HBM = pl.BlockSpec(memory_space=pltpu.HBM)


def exact(left, right, dims):
    return lax.dot_general(left, right, dims, precision=HIGHEST, preferred_element_type=jnp.float32)


def terms(value, count):
    found = []
    for _ in range(count):
        term = value.astype(jnp.bfloat16)
        found.append(term)
        value = value - term.astype(jnp.float32)
    return found


def stacked(left, right, dims):
    return lax.dot_general(left, right, dims, preferred_element_type=jnp.float32)


def factor(tiles):
    size = tiles[0].shape[1]
    lane = lax.broadcasted_iota(jnp.int32, (1, size), 1)
    row_in_tile = lax.broadcasted_iota(jnp.int32, (8, 1), 0)
    lanes = lax.broadcasted_iota(jnp.int32, (8, size), 1)
    tiles = list(tiles)
    for at in range(len(tiles)):
        first = 8 * at
        inside = (lane >= first) & (lane < first + 8)
        columns = {h: [jnp.broadcast_to(tiles[h][:, first + j : first + j + 1], (8, size)) for j in range(8)] for h in range(at, len(tiles))}
        for h in range(at + 1, len(tiles)):
            tiles[h] = jnp.where(inside, 0.0, tiles[h])
        for r in range(8):
            k = first + r
            row = tiles[at][r : r + 1, :]
            unit = jnp.where(lane == k, 1.0, row)
            behind = jnp.where(inside & (lane > k), 0.0, unit)
            pivots = [columns[at][j][r : r + 1, :] for j in range(8)]
            over = 1.0 / pivots[r]
            for h in range(at, len(tiles)):
                if h == at and r == 7:
                    continue
                times = columns[h][r] * over
                for j in range(r + 1, 8):
                    columns[h][j] = columns[h][j] - times * pivots[j]
                if h == at:
                    below = row_in_tile > r
                    tiles[h] = jnp.where(below, jnp.where(lanes == k, 0.0, tiles[h]) - times * unit, tiles[h])
                else:
                    tiles[h] = tiles[h] - times * behind
    uppers, inverses = [], []
    for h, tile in enumerate(tiles):
        rows = row_in_tile + 8 * h
        pivot = jnp.sum(jnp.where(lanes == rows, tile, 0.0), axis=1, keepdims=True)
        root = jnp.sqrt(pivot)
        over = 1.0 / root
        uppers.append(jnp.where(lanes > rows, tile * over, jnp.where(lanes == rows, root, 0.0)))
        inverses.append(jnp.where(lanes < rows, tile * over, jnp.where(lanes == rows, over, 0.0)))
    return uppers, inverses


def greet(sizes):
    nx, ny, nz = sizes
    gx, gy, gz = lax.axis_index("gx"), lax.axis_index("gy"), lax.axis_index("gz")
    barrier = pltpu.get_barrier_semaphore()
    me = gx * ny + gy
    for step in range(1, nx * ny):
        peer = lax.rem(me + step, nx * ny)
        pl.semaphore_signal(barrier, inc=1, device_id=(peer // ny, lax.rem(peer, ny), gz), device_id_type=MESH)
    for step in range(1, nz):
        pl.semaphore_signal(barrier, inc=1, device_id=(gx, gy, lax.rem(gz + step, nz)), device_id_type=MESH)


def all_sum(sizes, send, landed, column, gathered, send_sem, recv_sem):
    nx, ny, nz = sizes
    group = nx * ny
    gx, gy, gz = lax.axis_index("gx"), lax.axis_index("gy"), lax.axis_index("gz")
    me = gx * ny + gy

    def plane_copy(src, dst, step, base):
        peer = lax.rem(me + step, group)
        return pltpu.make_async_remote_copy(
            src_ref=src(peer),
            dst_ref=dst,
            send_sem=send_sem.at[base + step],
            recv_sem=recv_sem.at[base + step],
            device_id=(peer // ny, lax.rem(peer, ny), gz),
            device_id_type=MESH,
        )

    out = [plane_copy(lambda peer: send.at[peer], landed.at[step], step, 0) for step in range(1, group)]
    for copy in out:
        copy.start()
    part = send[me]
    for step in range(1, group):
        out[step - 1].wait_recv()
        part = part + landed[step]
    column[gz] = part
    along = [
        pltpu.make_async_remote_copy(
            src_ref=column.at[gz],
            dst_ref=column.at[gz],
            send_sem=send_sem.at[group + step],
            recv_sem=recv_sem.at[group + step],
            device_id=(gx, gy, lax.rem(gz + step, nz)),
            device_id_type=MESH,
        )
        for step in range(1, nz)
    ]
    for copy in along:
        copy.start()
    for copy in along:
        copy.wait_recv()
    total = column[0]
    for z in range(1, nz):
        total = total + column[z]
    gathered[me] = total
    back = [plane_copy(lambda peer: gathered.at[me], gathered.at[me], step, group + nz) for step in range(1, group)]
    for copy in back:
        copy.start()
    for copy in back:
        copy.wait_recv()
    for copy in out + along + back:
        copy.wait_send()


def sum_scratch(sizes, rows, size):
    nx, ny, nz = sizes
    group = nx * ny
    return [
        pltpu.VMEM((group, rows, size), jnp.float32),
        pltpu.VMEM((group, rows, size), jnp.float32),
        pltpu.VMEM((nz, rows, size), jnp.float32),
        pltpu.SemaphoreType.DMA((2 * group + nz,)),
        pltpu.SemaphoreType.DMA((2 * group + nz,)),
    ]


def chunk_of(width, most):
    return most if width % most == 0 else width


def reduce_kernel(sizes, panel, trailing, first, upper, summed, panel_held, trailing_held, first_held, move_sem, upper_held, *scratch):
    size, width = panel.shape
    trail = trailing.shape[0]
    group = sizes[0] * sizes[1]
    rows, less = size // group, trail // group
    chunk = chunk_of(width, 1024)
    greet(sizes)
    loads, more, stores = [], [], []
    for i in range(width // chunk):
        at = pl.ds(i * chunk, chunk)
        loads.append(pltpu.make_async_copy(panel.at[:, at], panel_held.at[:, at], move_sem.at[0, i]))
        loads[-1].start()
    for i in range(width // chunk):
        at = pl.ds(i * chunk, chunk)
        more.append(pltpu.make_async_copy(trailing.at[:, at], trailing_held.at[:, at], move_sem.at[1, i]))
        more[-1].start()
    both = jnp.zeros((2 * size, 2 * size), jnp.float32)
    small = jnp.zeros((size, size), jnp.float32)
    for i in range(width // chunk):
        loads[i].wait()
        high, middle, low = terms(panel_held[:, i * chunk : (i + 1) * chunk], 3)
        pair = jnp.concatenate([high, middle], axis=0)
        both = both + stacked(pair, pair, NT)
        small = small + stacked(high, low, NT)
    small = small + both[:size, size:]
    gram = both[:size, :size] + ((small + small.T) + both[size:, size:])
    gathered, *first_sum = scratch[:6]
    for p in range(group):
        first_sum[0][p] = gram[p * rows : (p + 1) * rows]
    pl.semaphore_wait(pltpu.get_barrier_semaphore(), group - 1 + sizes[2] - 1)
    all_sum(sizes, first_sum[0], first_sum[1], first_sum[2], gathered, *first_sum[3:])
    gram = jnp.concatenate([gathered[p] for p in range(group)], axis=0)
    uppers, inverses = factor([gram[h : h + 8] for h in range(0, size, 8)])
    for h in range(len(uppers)):
        upper_held[8 * h : 8 * h + 8] = uppers[h]
    stores.append(pltpu.make_async_copy(upper_held, upper, move_sem.at[3, 0]))
    stores[-1].start()
    inverse = jnp.concatenate(inverses, axis=0)
    one, two, three = terms(inverse, 3)
    left = jnp.concatenate([three, one, two, two, one, one], axis=1)
    total = jnp.zeros((size + 2 * trail, 2 * size), jnp.float32)
    for i in range(width // chunk):
        at = pl.ds(i * chunk, chunk)
        high, middle, low = terms(panel_held[:, at], 3)
        basis = stacked(left, jnp.concatenate([high, low, middle, high, middle, high], axis=0), NN)
        first_held[:, at] = basis
        stores.append(pltpu.make_async_copy(first_held.at[:, at], first.at[:, at], move_sem.at[2, i]))
        stores[-1].start()
        high, low = terms(basis, 2)
        more[i].wait()
        c_high, c_low = terms(trailing_held[:, at], 2)
        left_terms = jnp.concatenate([high, c_high, c_low], axis=0)
        total = total + stacked(left_terms, jnp.concatenate([high, low], axis=0), NT)
    mixed = total[:size, size:]
    own = total[:size, :size] + (mixed + mixed.T)
    cross = total[size:, :size] + total[size:, size:]
    cross = cross[:trail] + cross[trail:]
    second_sum = scratch[6:]
    for p in range(group):
        second_sum[0][p, :rows] = own[p * rows : (p + 1) * rows]
        second_sum[0][p, rows:] = cross[p * less : (p + 1) * less]
    all_sum(sizes, second_sum[0], second_sum[1], second_sum[2], summed, *second_sum[3:])
    for store in stores:
        store.wait()


def final_kernel(scale, summed, upper_one, first, trailing, basis, upper, coupling, updated, first_held, trailing_held, basis_held, updated_held, one_held, upper_held, coupling_held, load_sem, store_sem):
    size, width = first.shape
    loads = [
        pltpu.make_async_copy(first, first_held, load_sem.at[0]),
        pltpu.make_async_copy(trailing, trailing_held, load_sem.at[1]),
        pltpu.make_async_copy(upper_one, one_held, load_sem.at[2]),
    ]
    for load in loads:
        load.start()
    group = summed.shape[0]
    rows = size // group
    gram = jnp.concatenate([summed[p, :rows] for p in range(group)], axis=0)
    cross = jnp.concatenate([summed[p, rows:] for p in range(group)], axis=0)
    uppers, inverses = factor([gram[h : h + 8] for h in range(0, size, 8)])
    inv = jnp.concatenate(inverses, axis=0)
    up = jnp.concatenate(uppers, axis=0)
    mixed = exact(cross, inv, NT)
    coupling_held[...] = mixed
    both = jnp.concatenate([inv * scale, exact(mixed, inv, NN)], axis=0)
    high, low = terms(both, 2)
    left = jnp.concatenate([low, low, high, high], axis=1)
    chunk = chunk_of(width, 512)
    stores = [pltpu.make_async_copy(coupling_held, coupling, load_sem.at[3])]
    stores[0].start()
    for load in loads:
        load.wait()
    upper_held[...] = exact(up, one_held[...], NN) * (1.0 / scale)
    stores.append(pltpu.make_async_copy(upper_held, upper, load_sem.at[4]))
    stores[-1].start()
    for i in range(width // chunk):
        at = pl.ds(i * chunk, chunk)
        high, low = terms(first_held[:, at], 2)
        out = stacked(left, jnp.concatenate([low, high, low, high], axis=0), NN)
        basis_held[:, at] = out[:size]
        updated_held[:, at] = trailing_held[:, at] - out[size:]
        for place, (src, dst) in enumerate(((basis_held, basis), (updated_held, updated))):
            stores.append(pltpu.make_async_copy(src.at[:, at], dst.at[:, at], store_sem.at[place, i]))
            stores[-1].start()
    for store in stores:
        store.wait()


def shards(sizes, panel, trailing):
    size, width = panel.shape
    trail = trailing.shape[0]
    nx, ny, nz = sizes
    group = nx * ny
    rows, less = size // group, trail // group
    f32 = jnp.float32
    scale = float(width * group * nz) ** 0.5

    def params(identity=None, mebibytes=53):
        return pltpu.CompilerParams(
            collective_id=identity, has_side_effects=identity is not None, vmem_limit_bytes=mebibytes * 2**20
        )

    first, upper_one, summed = pl.pallas_call(
        functools.partial(reduce_kernel, sizes),
        out_shape=[
            jax.ShapeDtypeStruct((size, width), f32),
            jax.ShapeDtypeStruct((size, size), f32),
            jax.ShapeDtypeStruct((group, rows + less, size), f32),
        ],
        in_specs=[HBM, HBM],
        out_specs=[HBM, HBM, VMEM],
        scratch_shapes=[
            pltpu.VMEM((size, width), f32),
            pltpu.VMEM((trail, width), f32),
            pltpu.VMEM((size, width), f32),
            pltpu.SemaphoreType.DMA((4, width // chunk_of(width, 1024))),
            pltpu.VMEM((size, size), f32),
            pltpu.VMEM((group, rows, size), f32),
            *sum_scratch(sizes, rows, size),
            *sum_scratch(sizes, rows + less, size),
        ],
        compiler_params=params(0),
        name="reduce",
    )(panel, trailing)
    basis, upper, coupling_t, updated = pl.pallas_call(
        functools.partial(final_kernel, scale),
        out_shape=[
            jax.ShapeDtypeStruct((size, width), f32),
            jax.ShapeDtypeStruct((size, size), f32),
            jax.ShapeDtypeStruct((trail, size), f32),
            jax.ShapeDtypeStruct((trail, width), f32),
        ],
        in_specs=[VMEM, HBM, HBM, HBM],
        out_specs=[HBM] * 4,
        scratch_shapes=[
            pltpu.VMEM((size, width), f32),
            pltpu.VMEM((trail, width), f32),
            pltpu.VMEM((size, width), f32),
            pltpu.VMEM((trail, width), f32),
            pltpu.VMEM((size, size), f32),
            pltpu.VMEM((size, size), f32),
            pltpu.VMEM((trail, size), f32),
            pltpu.SemaphoreType.DMA((5,)),
            pltpu.SemaphoreType.DMA((2, width // chunk_of(width, 512))),
        ],
        compiler_params=params(),
        name="final",
    )(summed, upper_one, first, trailing)
    return basis, upper, coupling_t.T, updated


def solution(mesh):
    sizes = tuple(mesh.shape[name] for name in ("gx", "gy", "gz"))
    placed = P(None, ("gx", "gy", "gz"))
    return jax.shard_map(
        functools.partial(shards, sizes),
        mesh=mesh,
        in_specs=(placed, placed),
        out_specs=(placed, P(), P(), placed),
        check_vma=False,
    )
```

```python
import functools

import jax
import jax.numpy as jnp
from jax import lax
from jax.experimental import pallas as pl
from jax.experimental.pallas import tpu as pltpu
from jax.sharding import PartitionSpec as P

MESH = pl.DeviceIdType.MESH
HIGHEST = lax.Precision.HIGHEST
NT = (((1,), (1,)), ((), ()))
NN = (((1,), (0,)), ((), ()))
VMEM = pl.BlockSpec(memory_space=pltpu.VMEM)
HBM = pl.BlockSpec(memory_space=pltpu.HBM)


def exact(left, right, dims):
    return lax.dot_general(left, right, dims, precision=HIGHEST, preferred_element_type=jnp.float32)


def terms(value, count):
    found = []
    for _ in range(count):
        term = value.astype(jnp.bfloat16)
        found.append(term)
        value = value - term.astype(jnp.float32)
    return found


def stacked(left, right, dims):
    return lax.dot_general(left, right, dims, preferred_element_type=jnp.float32)


def factor(tiles):
    size = tiles[0].shape[1]
    lane = lax.broadcasted_iota(jnp.int32, (1, size), 1)
    row_in_tile = lax.broadcasted_iota(jnp.int32, (8, 1), 0)
    lanes = lax.broadcasted_iota(jnp.int32, (8, size), 1)
    tiles = list(tiles)
    for at in range(len(tiles)):
        first = 8 * at
        inside = (lane >= first) & (lane < first + 8)
        columns = {h: [jnp.broadcast_to(tiles[h][:, first + j : first + j + 1], (8, size)) for j in range(8)] for h in range(at, len(tiles))}
        for h in range(at + 1, len(tiles)):
            tiles[h] = jnp.where(inside, 0.0, tiles[h])
        for r in range(8):
            k = first + r
            row = tiles[at][r : r + 1, :]
            unit = jnp.where(lane == k, 1.0, row)
            behind = jnp.where(inside & (lane > k), 0.0, unit)
            pivots = [columns[at][j][r : r + 1, :] for j in range(8)]
            over = 1.0 / pivots[r]
            for h in range(at, len(tiles)):
                if h == at and r == 7:
                    continue
                times = columns[h][r] * over
                for j in range(r + 1, 8):
                    columns[h][j] = columns[h][j] - times * pivots[j]
                if h == at:
                    below = row_in_tile > r
                    tiles[h] = jnp.where(below, jnp.where(lanes == k, 0.0, tiles[h]) - times * unit, tiles[h])
                else:
                    tiles[h] = tiles[h] - times * behind
    uppers, inverses = [], []
    for h, tile in enumerate(tiles):
        rows = row_in_tile + 8 * h
        pivot = jnp.sum(jnp.where(lanes == rows, tile, 0.0), axis=1, keepdims=True)
        root = jnp.sqrt(pivot)
        over = 1.0 / root
        uppers.append(jnp.where(lanes > rows, tile * over, jnp.where(lanes == rows, root, 0.0)))
        inverses.append(jnp.where(lanes < rows, tile * over, jnp.where(lanes == rows, over, 0.0)))
    return uppers, inverses


def greet(sizes):
    nx, ny, nz = sizes
    gx, gy, gz = lax.axis_index("gx"), lax.axis_index("gy"), lax.axis_index("gz")
    barrier = pltpu.get_barrier_semaphore()
    me = gx * ny + gy
    for step in range(1, nx * ny):
        peer = lax.rem(me + step, nx * ny)
        pl.semaphore_signal(barrier, inc=1, device_id=(peer // ny, lax.rem(peer, ny), gz), device_id_type=MESH)
    for step in range(1, nz):
        pl.semaphore_signal(barrier, inc=1, device_id=(gx, gy, lax.rem(gz + step, nz)), device_id_type=MESH)


def all_sum(sizes, send, landed, column, gathered, send_sem, recv_sem):
    nx, ny, nz = sizes
    group = nx * ny
    gx, gy, gz = lax.axis_index("gx"), lax.axis_index("gy"), lax.axis_index("gz")
    me = gx * ny + gy

    def plane_copy(src, dst, step, base):
        peer = lax.rem(me + step, group)
        return pltpu.make_async_remote_copy(
            src_ref=src(peer),
            dst_ref=dst,
            send_sem=send_sem.at[base + step],
            recv_sem=recv_sem.at[base + step],
            device_id=(peer // ny, lax.rem(peer, ny), gz),
            device_id_type=MESH,
        )

    out = [plane_copy(lambda peer: send.at[peer], landed.at[step], step, 0) for step in range(1, group)]
    for copy in out:
        copy.start()
    part = send[me]
    for step in range(1, group):
        out[step - 1].wait_recv()
        part = part + landed[step]
    column[gz] = part
    along = [
        pltpu.make_async_remote_copy(
            src_ref=column.at[gz],
            dst_ref=column.at[gz],
            send_sem=send_sem.at[group + step],
            recv_sem=recv_sem.at[group + step],
            device_id=(gx, gy, lax.rem(gz + step, nz)),
            device_id_type=MESH,
        )
        for step in range(1, nz)
    ]
    for copy in along:
        copy.start()
    for copy in along:
        copy.wait_recv()
    total = column[0]
    for z in range(1, nz):
        total = total + column[z]
    gathered[me] = total
    back = [plane_copy(lambda peer: gathered.at[me], gathered.at[me], step, group + nz) for step in range(1, group)]
    for copy in back:
        copy.start()
    for copy in back:
        copy.wait_recv()
    for copy in out + along + back:
        copy.wait_send()


def sum_scratch(sizes, rows, size):
    nx, ny, nz = sizes
    group = nx * ny
    return [
        pltpu.VMEM((group, rows, size), jnp.float32),
        pltpu.VMEM((group, rows, size), jnp.float32),
        pltpu.VMEM((nz, rows, size), jnp.float32),
        pltpu.SemaphoreType.DMA((2 * group + nz,)),
        pltpu.SemaphoreType.DMA((2 * group + nz,)),
    ]


def chunk_of(width, most):
    return most if width % most == 0 else width


def reduce_kernel(sizes, panel, trailing, first, upper, summed, panel_held, trailing_held, first_held, move_sem, upper_held, *scratch):
    size, width = panel.shape
    trail = trailing.shape[0]
    group = sizes[0] * sizes[1]
    rows, less = size // group, trail // group
    chunk = chunk_of(width, 1024)
    loads, more, stores = [], [], []
    for i in range(width // chunk):
        at = pl.ds(i * chunk, chunk)
        loads.append(pltpu.make_async_copy(panel.at[:, at], panel_held.at[:, at], move_sem.at[0, i]))
        loads[-1].start()
    for i in range(width // chunk):
        at = pl.ds(i * chunk, chunk)
        more.append(pltpu.make_async_copy(trailing.at[:, at], trailing_held.at[:, at], move_sem.at[1, i]))
        more[-1].start()
    greet(sizes)
    both = jnp.zeros((2 * size, 2 * size), jnp.float32)
    small = jnp.zeros((size, size), jnp.float32)
    for i in range(width // chunk):
        loads[i].wait()
        high, middle, low = terms(panel_held[:, i * chunk : (i + 1) * chunk], 3)
        pair = jnp.concatenate([high, middle], axis=0)
        both = both + stacked(pair, pair, NT)
        small = small + stacked(high, low, NT)
    small = small + both[:size, size:]
    gram = both[:size, :size] + ((small + small.T) + both[size:, size:])
    gathered, *first_sum = scratch[:6]
    for p in range(group):
        first_sum[0][p] = gram[p * rows : (p + 1) * rows]
    pl.semaphore_wait(pltpu.get_barrier_semaphore(), group - 1 + sizes[2] - 1)
    all_sum(sizes, first_sum[0], first_sum[1], first_sum[2], gathered, *first_sum[3:])
    gram = jnp.concatenate([gathered[p] for p in range(group)], axis=0)
    uppers, inverses = factor([gram[h : h + 8] for h in range(0, size, 8)])
    for h in range(len(uppers)):
        upper_held[8 * h : 8 * h + 8] = uppers[h]
    stores.append(pltpu.make_async_copy(upper_held, upper, move_sem.at[3, 0]))
    stores[-1].start()
    inverse = jnp.concatenate(inverses, axis=0)
    one, two, three = terms(inverse, 3)
    left = jnp.concatenate([three, one, two, two, one, one], axis=1)
    total = jnp.zeros((size + 2 * trail, 2 * size), jnp.float32)
    for i in range(width // chunk):
        at = pl.ds(i * chunk, chunk)
        high, middle, low = terms(panel_held[:, at], 3)
        basis = stacked(left, jnp.concatenate([high, low, middle, high, middle, high], axis=0), NN)
        first_held[:, at] = basis
        stores.append(pltpu.make_async_copy(first_held.at[:, at], first.at[:, at], move_sem.at[2, i]))
        stores[-1].start()
        high, low = terms(basis, 2)
        more[i].wait()
        c_high, c_low = terms(trailing_held[:, at], 2)
        left_terms = jnp.concatenate([high, c_high, c_low], axis=0)
        total = total + stacked(left_terms, jnp.concatenate([high, low], axis=0), NT)
    mixed = total[:size, size:]
    own = total[:size, :size] + (mixed + mixed.T)
    cross = total[size:, :size] + total[size:, size:]
    cross = cross[:trail] + cross[trail:]
    second_sum = scratch[6:]
    for p in range(group):
        second_sum[0][p, :rows] = own[p * rows : (p + 1) * rows]
        second_sum[0][p, rows:] = cross[p * less : (p + 1) * less]
    all_sum(sizes, second_sum[0], second_sum[1], second_sum[2], summed, *second_sum[3:])
    for store in stores:
        store.wait()


def final_kernel(scale, summed, upper_one, first, trailing, basis, upper, coupling, updated, first_held, trailing_held, basis_held, updated_held, one_held, upper_held, coupling_held, load_sem, store_sem):
    size, width = first.shape
    loads = [
        pltpu.make_async_copy(first, first_held, load_sem.at[0]),
        pltpu.make_async_copy(trailing, trailing_held, load_sem.at[1]),
        pltpu.make_async_copy(upper_one, one_held, load_sem.at[2]),
    ]
    for load in loads:
        load.start()
    group = summed.shape[0]
    rows = size // group
    gram = jnp.concatenate([summed[p, :rows] for p in range(group)], axis=0)
    cross = jnp.concatenate([summed[p, rows:] for p in range(group)], axis=0)
    uppers, inverses = factor([gram[h : h + 8] for h in range(0, size, 8)])
    inv = jnp.concatenate(inverses, axis=0)
    up = jnp.concatenate(uppers, axis=0)
    mixed = exact(cross, inv, NT)
    coupling_held[...] = mixed
    both = jnp.concatenate([inv * scale, exact(mixed, inv, NN)], axis=0)
    high, low = terms(both, 2)
    left = jnp.concatenate([low, low, high, high], axis=1)
    chunk = chunk_of(width, 512)
    stores = [pltpu.make_async_copy(coupling_held, coupling, load_sem.at[3])]
    stores[0].start()
    for load in loads:
        load.wait()
    upper_held[...] = exact(up, one_held[...], NN) * (1.0 / scale)
    stores.append(pltpu.make_async_copy(upper_held, upper, load_sem.at[4]))
    stores[-1].start()
    for i in range(width // chunk):
        at = pl.ds(i * chunk, chunk)
        high, low = terms(first_held[:, at], 2)
        out = stacked(left, jnp.concatenate([low, high, low, high], axis=0), NN)
        basis_held[:, at] = out[:size]
        updated_held[:, at] = trailing_held[:, at] - out[size:]
        for place, (src, dst) in enumerate(((basis_held, basis), (updated_held, updated))):
            stores.append(pltpu.make_async_copy(src.at[:, at], dst.at[:, at], store_sem.at[place, i]))
            stores[-1].start()
    for store in stores:
        store.wait()


def shards(sizes, panel, trailing):
    size, width = panel.shape
    trail = trailing.shape[0]
    nx, ny, nz = sizes
    group = nx * ny
    rows, less = size // group, trail // group
    f32 = jnp.float32
    scale = float(width * group * nz) ** 0.5

    def params(identity=None, mebibytes=53):
        return pltpu.CompilerParams(
            collective_id=identity, has_side_effects=identity is not None, vmem_limit_bytes=mebibytes * 2**20
        )

    first, upper_one, summed = pl.pallas_call(
        functools.partial(reduce_kernel, sizes),
        out_shape=[
            jax.ShapeDtypeStruct((size, width), f32),
            jax.ShapeDtypeStruct((size, size), f32),
            jax.ShapeDtypeStruct((group, rows + less, size), f32),
        ],
        in_specs=[HBM, HBM],
        out_specs=[HBM, HBM, VMEM],
        scratch_shapes=[
            pltpu.VMEM((size, width), f32),
            pltpu.VMEM((trail, width), f32),
            pltpu.VMEM((size, width), f32),
            pltpu.SemaphoreType.DMA((4, width // chunk_of(width, 1024))),
            pltpu.VMEM((size, size), f32),
            pltpu.VMEM((group, rows, size), f32),
            *sum_scratch(sizes, rows, size),
            *sum_scratch(sizes, rows + less, size),
        ],
        compiler_params=params(0),
        name="reduce",
    )(panel, trailing)
    basis, upper, coupling_t, updated = pl.pallas_call(
        functools.partial(final_kernel, scale),
        out_shape=[
            jax.ShapeDtypeStruct((size, width), f32),
            jax.ShapeDtypeStruct((size, size), f32),
            jax.ShapeDtypeStruct((trail, size), f32),
            jax.ShapeDtypeStruct((trail, width), f32),
        ],
        in_specs=[VMEM, HBM, HBM, HBM],
        out_specs=[HBM] * 4,
        scratch_shapes=[
            pltpu.VMEM((size, width), f32),
            pltpu.VMEM((trail, width), f32),
            pltpu.VMEM((size, width), f32),
            pltpu.VMEM((trail, width), f32),
            pltpu.VMEM((size, size), f32),
            pltpu.VMEM((size, size), f32),
            pltpu.VMEM((trail, size), f32),
            pltpu.SemaphoreType.DMA((5,)),
            pltpu.SemaphoreType.DMA((2, width // chunk_of(width, 512))),
        ],
        compiler_params=params(),
        name="final",
    )(summed, upper_one, first, trailing)
    return basis, upper, coupling_t.T, updated


def solution(mesh):
    sizes = tuple(mesh.shape[name] for name in ("gx", "gy", "gz"))
    placed = P(None, ("gx", "gy", "gz"))
    return jax.shard_map(
        functools.partial(shards, sizes),
        mesh=mesh,
        in_specs=(placed, placed),
        out_specs=(placed, P(), P(), placed),
        check_vma=False,
    )
```
